256 devices in a mesh: tm: 8 (over y, core), graph: 32 (over x, z).
Axes of the slice: x: 4, y: 4, z: 8, core: 2. Of those that a mesh axis runs over, the one named last changes fastest.
Arguments:
- node_feats: bfloat16 [2, 8, 8192, 128], P(None, 'tm', 'graph'), may hold values from -6 to 6
- adjacency: bfloat16 [8, 64, 4, 128, 128], P('tm', 'graph'), may hold values from -0.25 to 0.25
- columns: int32 [8, 64, 4], P('tm', 'graph'), may hold values from 0 to 5, as said below
- send_list: int32 [8, 32, 4], P('tm', 'graph'), may hold values from 0 to 1
- w_input: bfloat16 [2, 128, 1536], replicated, may hold values from -0.5 to 0.5
- w_hidden: bfloat16 [2, 512, 1024], replicated, may hold values from -0.25 to 0.25
- w_cand: bfloat16 [2, 512, 512], replicated, may hold values from -0.25 to 0.25
- gate_bias: float32 [1536], replicated, may hold values from -3 to 3
Outputs:
- hidden_states: bfloat16 [2, 8, 8192, 512], P(None, 'tm', 'graph')
The draws below stay inside these ranges and needn't reach their ends.
Inputs may be any that keep to these rules, and one draw needn't show every extreme that they name: `columns`: A row tile's 4 codes are distinct, and the 2 row tiles of a partition together use every code in each snapshot.
All inputs are finite; a program needn't handle non-finite values.
Results may differ from the reference program's by a relative error of at most 0.0038.
Values may be sent and summed in bfloat16 or wider, within the bound.
No kernel may reach another device: no remote copies, remote signals or barrier semaphores. Data moves between devices by JAX's collectives and lax.ppermute only.
A program may use at most 64 MiB of HBM per device.

```python
import jax
import jax.numpy as jnp

HID = 512
FEAT = 128
BLK = 128
KB = 4
LB = 2
SEQS = 2
SNAPS = 8
PARTS_SIZE = 32
BLOCKS = 64
VERTS = 8192
CODES = 6


def draw_columns(key, part):
    key_list = jax.random.split(jax.random.fold_in(key, 11), SNAPS * PARTS_SIZE)
    orders = jax.vmap(lambda single: jax.random.permutation(single, CODES))(key_list)
    leading = orders[:, :KB]
    second = orders[:, CODES - KB:]
    tile_codes = jnp.stack([leading, second], axis=1)
    return tile_codes.reshape(SNAPS, PARTS_SIZE * LB, KB).astype(jnp.int32)


def with_ends(values, rng, low, top_value):
    longest = values.shape.index(max(values.shape))
    spots = []
    for shift in (0, 1):
        where = [jax.random.randint(jax.random.fold_in(rng, axis), (), 0, length) for axis, length in enumerate(values.shape)]
        where[longest] = (where[longest] + shift) % values.shape[longest]
        spots.append(tuple(where))
    return values.at[spots[0]].set(low).at[spots[1]].set(top_value)


def block_levels(stream_key, shape, cuts, smallest, largest):
    loudness, own = 1.0, jax.random.fold_in(stream_key, 6)
    for axis_at, parts in cuts:
        draws = jnp.exp(jax.random.uniform(jax.random.fold_in(own, axis_at), (parts,), jnp.float32, smallest / len(cuts), largest / len(cuts)))
        loudness = loudness * jnp.repeat(draws, shape[axis_at] // parts).reshape([-1 if axis == axis_at else 1 for axis in range(len(shape))])
    return loudness


def bell_draw(rng, shape, spread, most, shards=(), held_as=jnp.bfloat16):
    values = spread * jax.random.normal(rng, shape, jnp.float32)
    if shards:
        values = values * block_levels(rng, shape, shards, -0.22, 0.18)
    return jnp.clip(values, -most, most).astype(held_as)


def setup_inputs(seed: int = 0) -> dict:
    seeds = jax.random.split(jax.random.key(seed), 9)
    return {
        "node_feats": bell_draw(seeds[0], (SEQS, SNAPS, VERTS, FEAT), 1.0, 6.0, ((1, 8), (2, 32))),
        "adjacency": bell_draw(seeds[1], (SNAPS, BLOCKS, KB, BLK, BLK), (KB * BLK) ** -0.5, 0.25, ((0, 8), (1, 32))),
        "columns": draw_columns(jax.random.fold_in(seeds[8], 71), 0),
        "send_list": with_ends(jax.random.randint(seeds[3], (SNAPS, PARTS_SIZE, 4), 0, LB), jax.random.fold_in(seeds[3], 1), 0, LB - 1).astype(jnp.int32),
        "w_input": bell_draw(seeds[4], (2, FEAT, 3 * HID), FEAT ** -0.5, 0.5),
        "w_hidden": bell_draw(seeds[5], (2, HID, 2 * HID), HID ** -0.5, 0.25),
        "w_cand": bell_draw(seeds[6], (2, HID, HID), HID ** -0.5, 0.25),
        "gate_bias": jnp.clip(jax.random.uniform(seeds[7], (3 * HID,), jnp.float32, -3.0, 3.0), -3.0, 3.0),
    }


OFFSETS = (-2, -1, 1, 2)


def column_blocks(columns, send_list):
    tile_ids = jnp.arange(BLOCKS, dtype=jnp.int32)
    part_ids = (tile_ids // LB)[None, :, None]
    position = jnp.clip(columns - LB, 0, 3).astype(jnp.int32)
    offset_now = jnp.array(OFFSETS, dtype=jnp.int32)[position]
    source = ((part_ids + offset_now) % PARTS_SIZE).astype(jnp.int32)
    snap_ids = jnp.arange(SNAPS, dtype=jnp.int32)[:, None, None]
    sent_block = send_list[snap_ids, source, 3 - position]
    return jnp.where(columns < LB, part_ids * LB + columns, source * LB + sent_block).astype(jnp.int32)


def operate(block_row, weights_now, values):
    blocks = values.reshape(BLOCKS, BLK, values.shape[1])
    picked = blocks[block_row]
    mixed = jnp.einsum("gkij,gkjw->giw", weights_now.astype(jnp.float32), picked.astype(jnp.float32))
    return mixed.reshape(VERTS, values.shape[1])


def reference(node_feats, adjacency, columns, send_list, w_input, w_hidden, w_cand, gate_bias):
    block_ids = column_blocks(columns, send_list)
    results = []
    for sequence in range(SEQS):
        hidden = jnp.zeros((VERTS, HID), jnp.bfloat16)
        states = []
        for snapshot in range(SNAPS):
            x_rows = node_feats[sequence, snapshot]
            mixed = operate(block_ids[snapshot], adjacency[snapshot], jnp.concatenate([x_rows, hidden], axis=1)).astype(jnp.bfloat16)
            mixed_x = mixed[:, :FEAT]
            mixed_h = mixed[:, FEAT:]
            input_part = jnp.dot(x_rows, w_input[0], preferred_element_type=jnp.float32) + jnp.dot(mixed_x, w_input[1], preferred_element_type=jnp.float32) + gate_bias
            hidden_part = jnp.dot(hidden, w_hidden[0], preferred_element_type=jnp.float32) + jnp.dot(mixed_h, w_hidden[1], preferred_element_type=jnp.float32)
            update_gate = jax.nn.sigmoid(input_part[:, :HID] + hidden_part[:, :HID])
            reset_gate = jax.nn.sigmoid(input_part[:, HID:2 * HID] + hidden_part[:, HID:])
            hidden_f = hidden.astype(jnp.float32)
            reset_state = (reset_gate * hidden_f).astype(jnp.bfloat16)
            reset_mixed = operate(block_ids[snapshot], adjacency[snapshot], reset_state).astype(jnp.bfloat16)
            candidate = jnp.tanh(input_part[:, 2 * HID:] + jnp.dot(reset_state, w_cand[0], preferred_element_type=jnp.float32) + jnp.dot(reset_mixed, w_cand[1], preferred_element_type=jnp.float32))
            hidden = (update_gate * hidden_f + (1.0 - update_gate) * candidate).astype(jnp.bfloat16)
            states.append(hidden)
        results.append(jnp.stack(states))
    return jnp.stack(results)
```

```python
import functools

import jax
import jax.numpy as jnp
from jax import lax
from jax.experimental import pallas as pl
from jax.experimental.pallas import tpu as pltpu
from jax.sharding import PartitionSpec as P

OFFSETS = (-2, -1, 1, 2)
AXES = ("tm", "graph")
PARTS, BLK, HID, FEAT = 32, 128, 512, 128
ROWS = 2 * BLK
CYCLE = (
    (2, 2), (2, 1), (2, 0), (3, 0), (3, 1), (3, 2), (3, 3), (2, 3),
    (1, 3), (0, 3), (0, 2), (0, 1), (0, 0), (1, 0), (1, 1), (1, 2),
)
LADDER = ((0, 0), (0, 1), (1, 1), (1, 0))


def place(seq, pair, part):
    x, y = CYCLE[part // 2]
    plane_pair, core = LADDER[pair]
    z = 4 * seq + 2 * plane_pair + 1 - part % 2
    return (2 * y + core) * PARTS + x * 8 + z


EVERY = [(s, q, p) for s in range(2) for q in range(4) for p in range(PARTS)]


def exchange_route(offset, swap):
    return [(place(s, q, p), place(s, q ^ swap, (p - offset) % PARTS)) for s, q, p in EVERY]


def input_route(other):
    return [((2 * q + (s ^ other)) * PARTS + p, place(s, q, p)) for s, q, p in EVERY]


def completed(route):
    to, came = dict(route), {b: a for a, b in route}
    for first in sorted(set(to) - set(came)):
        end = first
        while end in to:
            end = to[end]
        to[end], came[first] = first, end
    idle = [d for d in range(8 * PARTS) if d not in to]
    spare = []
    for d in idle:
        sibling = d ^ PARTS
        if sibling not in idle:
            spare.append(d)
        else:
            to[d] = sibling
    if len(spare) == 1:
        a = next(d for d in idle if d in to)
        to[spare[0]], to[a] = to[a], spare[0]
    else:
        for a, b in zip(spare, spare[1:] + spare[:1]):
            to[a] = b
    return sorted(to.items())


def output_route(snaps, other):
    route = []
    for t in snaps:
        pair = t // 2 if t < 4 else 3 - t // 2
        route += [(place((t % 2) ^ other, pair, p), t * PARTS + p) for p in range(PARTS)]
    return completed(route)


INPUT, SMALL, MIXED, NEXT, TOTAL = 1024, 1280, 1296, 1552, 1568
SEND, PAIR = 8, 12

VMEM = pl.BlockSpec(memory_space=pltpu.VMEM)
SMEM = pl.BlockSpec(memory_space=pltpu.SMEM)


def call(body, table, operands, outs, flops, scratch=(), aliases=None):
    shapes = [jax.ShapeDtypeStruct(shape, dtype) for shape, dtype in outs]
    size = sum(v.size * v.dtype.itemsize for v in (*operands, *shapes))
    return pl.pallas_call(
        body,
        out_shape=shapes,
        in_specs=[SMEM] + [VMEM] * len(operands),
        out_specs=[VMEM] * len(outs),
        scratch_shapes=list(scratch),
        input_output_aliases=aliases or {},
        compiler_params=pltpu.CompilerParams(vmem_limit_bytes=12 << 20),
        cost_estimate=pl.CostEstimate(flops=flops, bytes_accessed=size, transcendentals=0),
    )(table, *operands)


def dot(a, b):
    return jnp.dot(a, b, preferred_element_type=jnp.float32)


def graph_product(table, row, source, slots, out):
    @pl.loop(0, 2)
    def _(tile):
        at = pl.multiple_of(tile * 4 * BLK, 4 * BLK)
        weights = jnp.concatenate([source[pl.ds(at + k * BLK, BLK), :] for k in range(4)], axis=1)
        picked = jnp.concatenate([slots[table[row, 4 * tile + k]] for k in range(4)], axis=0)
        out[pl.ds(pl.multiple_of(tile * BLK, BLK), BLK), :] = dot(weights, picked).astype(jnp.bfloat16)


def fill(slots, own, halos):
    slots[0] = own[:BLK, :]
    slots[1] = own[BLK:, :]
    for i, halo in enumerate(halos):
        slots[2 + i] = halo[...]


def put_toward(table, row, own, toward):
    for i, out in enumerate(toward):
        start = pl.multiple_of(table[row, SEND + 3 - i] * BLK, BLK)
        out[...] = own[pl.ds(start, BLK), :]


def halves(body):
    @pl.loop(0, 2)
    def _(j):
        body(pl.multiple_of(j * 256, 256))


def toward_inputs(table, even, odd, *outs):
    *toward, small = outs
    for slot, source in enumerate((even, odd)):
        for i, out in enumerate(toward):
            start = pl.multiple_of(INPUT + table[slot, SEND + 3 - i] * BLK, BLK)
            out[slot * BLK : (slot + 1) * BLK, :] = source[pl.ds(start, BLK), :]
    small[...] = even[SMALL:, :]


def mix_inputs(table, even, odd, h0, h1, h2, h3, following, full_even, full_odd, slots):
    for slot, (source, out) in enumerate(((even, full_even), (odd, full_odd))):
        out[:MIXED, :] = source[...]
        out[NEXT:, :] = following[...]
        slots[0] = source[INPUT : INPUT + BLK, :]
        slots[1] = source[INPUT + BLK : SMALL, :]
        for i, halo in enumerate((h0, h1, h2, h3)):
            slots[2 + i] = halo[slot * BLK : (slot + 1) * BLK, :]
        graph_product(table, slot, source, slots, out.at[MIXED:NEXT])


def input_gate(source, w_input, bias, cols):
    return (
        dot(source[INPUT:SMALL, :], w_input[0, :, cols])
        + dot(source[MIXED:NEXT, :], w_input[1, :, cols])
        + bias[:, cols]
    )


def first_step(table, source, w_input, bias, hidden, t0, t1, t2, t3):
    def half(at):
        update = jax.nn.sigmoid(input_gate(source, w_input, bias, pl.ds(at, 256)))
        candidate = jnp.tanh(input_gate(source, w_input, bias, pl.ds(at + 2 * HID, 256)))
        hidden[:, pl.ds(at, 256)] = ((1.0 - update) * candidate).astype(jnp.bfloat16)

    halves(half)
    put_toward(table, 1, hidden, (t0, t1, t2, t3))


def early_gates(table, source, hidden, w_input, w_hidden, bias, gates):
    @pl.loop(0, 4)
    def _(j):
        cols = pl.ds(pl.multiple_of(j * 256, 256), 256)
        gates[:, cols] = input_gate(source, w_input, bias, cols) + dot(hidden[...], w_hidden[0, :, cols])

    @pl.loop(4, 6)
    def _(j):
        cols = pl.ds(pl.multiple_of(j * 256, 256), 256)
        gates[:, cols] = input_gate(source, w_input, bias, cols)


def reset_step(slot, table, hidden, h0, h1, h2, h3, source, gates, w_hidden, state, mixed, t0, t1, t2, t3, slots):
    fill(slots, hidden, (h0, h1, h2, h3))
    graph_product(table, slot, source, slots, mixed)

    def half(at):
        cols, here = pl.ds(at + HID, 256), pl.ds(at, 256)
        reset = jax.nn.sigmoid(gates[:, cols] + dot(mixed[...], w_hidden[1, :, cols]))
        state[:, here] = (reset * hidden[:, here].astype(jnp.float32)).astype(jnp.bfloat16)

    halves(half)
    put_toward(table, slot, state, (t0, t1, t2, t3))


def late_gates(table, gates, mixed, state, w_hidden, w_cand, update, partial):
    def half(at):
        here = pl.ds(at, 256)
        update[:, here] = jax.nn.sigmoid(gates[:, here] + dot(mixed[...], w_hidden[1, :, here]))
        partial[:, here] = gates[:, pl.ds(at + 2 * HID, 256)] + dot(state[...], w_cand[0, :, here])

    halves(half)


def new_hidden(slot, pair, last, table, hidden, state, h0, h1, h2, h3, source, update, partial, w_cand, kept_in, out, kept, *rest):
    *toward, slots, mixed = rest
    fill(slots, state, (h0, h1, h2, h3))
    graph_product(table, slot, source, slots, mixed)

    def half(at):
        here = pl.ds(at, 256)
        candidate = jnp.tanh(partial[:, here] + dot(mixed[...], w_cand[1, :, here]))
        gate = update[:, here]
        value = gate * hidden[:, here].astype(jnp.float32) + (1.0 - gate) * candidate
        out[:, here] = value.astype(jnp.bfloat16)

    halves(half)
    if not last:
        put_toward(table, 1 + slot, out, toward)

    @pl.when(table[0, PAIR] == pair)
    def _():
        kept[...] = out[...]


def local(node_feats, adjacency, columns, send_list, w_input, w_hidden, w_cand, gate_bias):
    bf16, f32 = jnp.bfloat16, jnp.float32
    snap = lax.axis_index("tm")
    z, core = lax.axis_index("graph") % 8, snap % 2
    seq, near = z // 4, (z % 4) < 2
    bias = gate_bias[None, :]
    small = jnp.concatenate([columns.reshape(-1), send_list.reshape(-1), jnp.full((116,), snap // 2, jnp.int32)])
    small = jnp.broadcast_to(small.astype(bf16)[None], (16, 128))
    feats = node_feats[:, 0]
    mine = jnp.where(core == 0, feats[0], feats[1])
    others = jnp.where(core == 0, feats[1], feats[0])
    weights = adjacency.reshape(8 * BLK, BLK)
    got = [
        lax.ppermute(jnp.concatenate([weights, x, small], axis=0), AXES, input_route(other))
        for x, other in ((mine, 0), (others, 1))
    ]
    even = jnp.where(seq == 0, got[0], got[1])
    odd = jnp.where(seq == 0, got[1], got[0])
    block = ((BLK, HID), bf16)
    full = ((ROWS, HID), bf16)
    wide = ((ROWS, HID), f32)
    buffer = ((TOTAL, BLK), bf16)
    slots = pltpu.VMEM((6, BLK, HID), bf16)

    def integers(*rows):
        return jnp.concatenate([r[:1] for r in rows], axis=0).astype(jnp.int32)

    def exchange(blocks, swap=0):
        return [lax.ppermute(b, AXES, exchange_route(o, swap)) for b, o in zip(blocks, OFFSETS)]

    table = integers(even[SMALL:], odd[SMALL:])
    *toward, small = call(
        toward_inputs, table, (even, odd), [((2 * BLK, FEAT), bf16)] * 4 + [((16, 128), bf16)], 0
    )
    following = lax.ppermute(small, AXES, exchange_route(0, 1))
    halos = exchange(toward)
    even, odd = call(
        mix_inputs, table, (even, odd, *halos, following), [buffer] * 2, 2 * 2 * ROWS * 512 * FEAT,
        scratch=(pltpu.VMEM((6, BLK, FEAT), bf16),),
    )
    hidden, *toward = call(
        first_step, table, (even, w_input, bias), [full] + [block] * 4, 2 * ROWS * 256 * 1024
    )
    away = [(place(s, q, p), place(s, 3 - q, p)) for s, q, p in EVERY]
    later = [lax.ppermute(v, AXES, away) for v in (even, odd)]
    tables = [
        integers(even[SMALL:], odd[SMALL:], even[NEXT:]),
        integers(even[SMALL:], odd[SMALL:], later[0][SMALL:]),
        integers(later[0][SMALL:], later[1][SMALL:], later[0][NEXT:]),
    ]
    kept = [[hidden, hidden], [hidden, hidden]]
    waves = []
    for t in range(1, 8):
        slot, swap = t % 2, int(t in (2, 6))
        source = (later if t >= 4 else (even, odd))[slot]
        table = tables[2 if t >= 4 else int(t == 3)]
        if swap:
            hidden = lax.ppermute(hidden, AXES, exchange_route(0, 1))
        halos = exchange(toward, swap)
        (gates,) = call(
            early_gates, table, (source, hidden, w_input, w_hidden, bias), [((ROWS, 3 * HID), f32)],
            2 * ROWS * (256 * 1536 + 512 * 1024),
        )
        state, mixed_h, *toward = call(
            functools.partial(reset_step, slot), table, (hidden, *halos, source, gates, w_hidden),
            [full, full] + [block] * 4, 2 * ROWS * 512 * 1024, scratch=(slots,),
        )
        halos = exchange(toward)
        update, partial = call(
            late_gates, table, (gates, mixed_h, state, w_hidden, w_cand), [wide, wide], 2 * ROWS * 512 * 1024
        )
        last, keep = t == 7, kept[t // 4]
        hidden, keep[slot], *toward = call(
            functools.partial(new_hidden, slot, t // 2, last), table,
            (hidden, state, *halos, source, update, partial, w_cand, keep[slot]),
            [full, full] + [block] * (0 if last else 4), 2 * ROWS * 512 * 1024,
            scratch=(slots, pltpu.VMEM((ROWS, HID), bf16)), aliases={11: 1},
        )
        if t == 3:
            waves.append([jnp.where(seq == 0, keep[o], keep[1 - o]) for o in range(2)])
        if t == 6:
            fifth = (core == LADDER[1][1]) & near
            waves.append([jnp.where(fifth & (seq != o), keep[1], keep[0]) for o in range(2)])
    waves.append([hidden, hidden])
    snaps = ((0, 1, 2, 3), (4, 5, 6), (7,))
    came = [
        [lax.ppermute(v, AXES, output_route(ts, o)) for o, v in enumerate(wave)] for ts, wave in zip(snaps, waves)
    ]
    first, second = [jnp.where(snap < 4, came[0][o], jnp.where(snap < 7, came[1][o], came[2][o])) for o in range(2)]
    flip = core == 0
    return jnp.stack([jnp.where(flip, first, second), jnp.where(flip, second, first)])[:, None]


def solution(mesh):
    return jax.shard_map(
        local,
        mesh=mesh,
        in_specs=(
            P(None, "tm", "graph", None),
            P("tm", "graph", None, None, None),
            P("tm", "graph", None),
            P("tm", "graph", None),
            P(),
            P(),
            P(),
            P(),
        ),
        out_specs=P(None, "tm", "graph", None),
        check_vma=False,
    )
```

```python
import functools

import jax
import jax.numpy as jnp
from jax import lax
from jax.experimental import pallas as pl
from jax.experimental.pallas import tpu as pltpu
from jax.sharding import PartitionSpec as P


OFFSETS = (-2, -1, 1, 2)
AXES = ("tm", "graph")
PARTS, BLK, HID, FEAT = 32, 128, 512, 128
ROWS = 2 * BLK
CYCLE = (
    (2, 2), (2, 1), (2, 0), (3, 0), (3, 1), (3, 2), (3, 3), (2, 3),
    (1, 3), (0, 3), (0, 2), (0, 1), (0, 0), (1, 0), (1, 1), (1, 2),
)
LADDER = ((0, 0), (0, 1), (1, 1), (1, 0))


def place(seq, pair, part):
    x, y = CYCLE[part // 2]
    plane_pair, core = LADDER[pair]
    z = 4 * seq + 2 * plane_pair + 1 - part % 2
    return (2 * y + core) * PARTS + x * 8 + z


EVERY = [(s, q, p) for s in range(2) for q in range(4) for p in range(PARTS)]


def exchange_route(offset, swap):
    return [(place(s, q, p), place(s, q ^ swap, (p - offset) % PARTS)) for s, q, p in EVERY]


def input_route(other):
    return [((2 * q + (s ^ other)) * PARTS + p, place(s, q, p)) for s, q, p in EVERY]


def completed(route):
    to, came = dict(route), {b: a for a, b in route}
    for first in sorted(set(to) - set(came)):
        end = first
        while end in to:
            end = to[end]
        to[end], came[first] = first, end
    idle = [d for d in range(8 * PARTS) if d not in to]
    spare = []
    for d in idle:
        sibling = d ^ PARTS
        if sibling not in idle:
            spare.append(d)
        else:
            to[d] = sibling
    if len(spare) == 1:
        a = next(d for d in idle if d in to)
        to[spare[0]], to[a] = to[a], spare[0]
    else:
        for a, b in zip(spare, spare[1:] + spare[:1]):
            to[a] = b
    return sorted(to.items())


def output_route(snaps, other):
    route = []
    for t in snaps:
        pair = t // 2 if t < 4 else 3 - t // 2
        route += [(place((t % 2) ^ other, pair, p), t * PARTS + p) for p in range(PARTS)]
    return completed(route)


INPUT, SMALL, MIXED, NEXT, TOTAL = 1024, 1280, 1296, 1552, 1568
SEND, PAIR = 8, 12

VMEM = pl.BlockSpec(memory_space=pltpu.VMEM)
SMEM = pl.BlockSpec(memory_space=pltpu.SMEM)


def call(body, table, operands, outs, flops, scratch=(), aliases=None):
    shapes = [jax.ShapeDtypeStruct(shape, dtype) for shape, dtype in outs]
    size = sum(v.size * v.dtype.itemsize for v in (*operands, *shapes))
    return pl.pallas_call(
        body,
        out_shape=shapes,
        in_specs=[SMEM] + [VMEM] * len(operands),
        out_specs=[VMEM] * len(outs),
        scratch_shapes=list(scratch),
        input_output_aliases=aliases or {},
        compiler_params=pltpu.CompilerParams(vmem_limit_bytes=12 << 20),
        cost_estimate=pl.CostEstimate(flops=flops, bytes_accessed=size, transcendentals=0),
    )(table, *operands)


def dot(a, b):
    return jnp.dot(a, b, preferred_element_type=jnp.float32)


def graph_product(table, row, source, slots, out):
    for tile in range(2):
        at = tile * 4 * BLK
        weights = jnp.concatenate([source[at + k * BLK : at + (k + 1) * BLK, :] for k in range(4)], axis=1)
        picked = jnp.concatenate([slots[table[row, 4 * tile + k]] for k in range(4)], axis=0)
        out[tile * BLK : (tile + 1) * BLK, :] = dot(weights, picked).astype(jnp.bfloat16)


def fill(slots, own, halos):
    slots[0] = own[:BLK, :]
    slots[1] = own[BLK:, :]
    for i, halo in enumerate(halos):
        slots[2 + i] = halo[...]


def put_toward(table, row, own, toward):
    for i, out in enumerate(toward):
        start = pl.multiple_of(table[row, SEND + 3 - i] * BLK, BLK)
        out[...] = own[pl.ds(start, BLK), :]


def toward_inputs(table, even, odd, *outs):
    *toward, small = outs
    for slot, source in enumerate((even, odd)):
        for i, out in enumerate(toward):
            start = pl.multiple_of(INPUT + table[slot, SEND + 3 - i] * BLK, BLK)
            out[slot * BLK : (slot + 1) * BLK, :] = source[pl.ds(start, BLK), :]
    small[...] = even[SMALL:, :]


def mix_inputs(table, even, odd, h0, h1, h2, h3, following, full_even, full_odd, slots):
    for slot, (source, out) in enumerate(((even, full_even), (odd, full_odd))):
        out[:MIXED, :] = source[...]
        out[NEXT:, :] = following[...]
        slots[0] = source[INPUT : INPUT + BLK, :]
        slots[1] = source[INPUT + BLK : SMALL, :]
        for i, halo in enumerate((h0, h1, h2, h3)):
            slots[2 + i] = halo[slot * BLK : (slot + 1) * BLK, :]
        graph_product(table, slot, source, slots, out.at[MIXED:NEXT])


def input_gate(source, w_input, bias, cols):
    return (
        dot(source[INPUT:SMALL, :], w_input[0, :, cols])
        + dot(source[MIXED:NEXT, :], w_input[1, :, cols])
        + bias[:, cols]
    )


def first_step(table, source, w_input, bias, hidden, t0, t1, t2, t3):
    update = jax.nn.sigmoid(input_gate(source, w_input, bias, slice(0, HID)))
    candidate = jnp.tanh(input_gate(source, w_input, bias, slice(2 * HID, 3 * HID)))
    hidden[...] = ((1.0 - update) * candidate).astype(jnp.bfloat16)
    put_toward(table, 1, hidden, (t0, t1, t2, t3))


def early_gates(table, source, hidden, w_input, w_hidden, bias, gates):
    for column in range(3):
        cols = slice(column * HID, (column + 1) * HID)
        value = input_gate(source, w_input, bias, cols)
        if column < 2:
            value += dot(hidden[...], w_hidden[0, :, cols])
        gates[:, cols] = value


def reset_step(slot, table, hidden, h0, h1, h2, h3, source, gates, w_hidden, state, mixed, t0, t1, t2, t3, slots):
    fill(slots, hidden, (h0, h1, h2, h3))
    graph_product(table, slot, source, slots, mixed)
    reset = jax.nn.sigmoid(gates[:, HID : 2 * HID] + dot(mixed[...], w_hidden[1, :, HID:]))
    state[...] = (reset * hidden[...].astype(jnp.float32)).astype(jnp.bfloat16)
    put_toward(table, slot, state, (t0, t1, t2, t3))


def late_gates(table, gates, mixed, state, w_hidden, w_cand, update, partial):
    update[...] = jax.nn.sigmoid(gates[:, :HID] + dot(mixed[...], w_hidden[1, :, :HID]))
    partial[...] = gates[:, 2 * HID :] + dot(state[...], w_cand[0])


def new_hidden(slot, pair, last, table, hidden, state, h0, h1, h2, h3, source, update, partial, w_cand, kept_in, out, kept, *rest):
    *toward, slots, mixed = rest
    fill(slots, state, (h0, h1, h2, h3))
    graph_product(table, slot, source, slots, mixed)
    candidate = jnp.tanh(partial[...] + dot(mixed[...], w_cand[1]))
    gate = update[...]
    out[...] = (gate * hidden[...].astype(jnp.float32) + (1.0 - gate) * candidate).astype(jnp.bfloat16)
    if not last:
        put_toward(table, 1 + slot, out, toward)

    @pl.when(table[0, PAIR] == pair)
    def _():
        kept[...] = out[...]


def local(node_feats, adjacency, columns, send_list, w_input, w_hidden, w_cand, gate_bias):
    bf16, f32 = jnp.bfloat16, jnp.float32
    snap = lax.axis_index("tm")
    z, core = lax.axis_index("graph") % 8, snap % 2
    seq = z // 4
    bias = gate_bias[None, :]
    small = jnp.concatenate([columns.reshape(-1), send_list.reshape(-1), jnp.full((116,), snap // 2, jnp.int32)])
    small = jnp.broadcast_to(small.astype(bf16)[None], (16, 128))
    feats = node_feats[:, 0]
    mine = jnp.where(core == 0, feats[0], feats[1])
    others = jnp.where(core == 0, feats[1], feats[0])
    weights = adjacency.reshape(8 * BLK, BLK)
    got = [
        lax.ppermute(jnp.concatenate([weights, x, small], axis=0), AXES, input_route(other))
        for x, other in ((mine, 0), (others, 1))
    ]
    even = jnp.where(seq == 0, got[0], got[1])
    odd = jnp.where(seq == 0, got[1], got[0])
    block = ((BLK, HID), bf16)
    full = ((ROWS, HID), bf16)
    wide = ((ROWS, HID), f32)
    buffer = ((TOTAL, BLK), bf16)
    slots = pltpu.VMEM((6, BLK, HID), bf16)

    def integers(*rows):
        return jnp.concatenate([r[:1] for r in rows], axis=0).astype(jnp.int32)

    def exchange(blocks, swap=0):
        return [lax.ppermute(b, AXES, exchange_route(o, swap)) for b, o in zip(blocks, OFFSETS)]

    table = integers(even[SMALL:], odd[SMALL:])
    *toward, small = call(
        toward_inputs, table, (even, odd), [((2 * BLK, FEAT), bf16)] * 4 + [((16, 128), bf16)], 0
    )
    following = lax.ppermute(small, AXES, exchange_route(0, 1))
    halos = exchange(toward)
    even, odd = call(
        mix_inputs, table, (even, odd, *halos, following), [buffer] * 2, 2 * 2 * ROWS * 512 * FEAT,
        scratch=(pltpu.VMEM((6, BLK, FEAT), bf16),),
    )
    hidden, *toward = call(
        first_step, table, (even, w_input, bias), [full] + [block] * 4, 2 * ROWS * 256 * 1024
    )
    away = [(place(s, q, p), place(s, 3 - q, p)) for s, q, p in EVERY]
    later = [lax.ppermute(v, AXES, away) for v in (even, odd)]
    table = integers(even[SMALL:], odd[SMALL:], even[NEXT:])
    kept = [[hidden, hidden], [hidden, hidden]]
    came = []
    for t in range(1, 8):
        slot, swap = t % 2, int(t in (2, 6))
        source = (later if t >= 4 else (even, odd))[slot]
        if t == 3:
            later[0], later[1], toward[0] = lax.optimization_barrier((later[0], later[1], toward[0]))
            table = integers(even[SMALL:], odd[SMALL:], later[0][SMALL:])
        if t == 4:
            table = integers(later[0][SMALL:], later[1][SMALL:], later[0][NEXT:])
        if swap:
            hidden = lax.ppermute(hidden, AXES, exchange_route(0, 1))
        halos = exchange(toward, swap)
        (gates,) = call(
          early_gates, table, (source, hidden, w_input, w_hidden, bias), [((ROWS, 3 * HID), f32)],
          2 * ROWS * (256 * 1536 + 512 * 1024),
        )
        state, mixed_h, *toward = call(
            functools.partial(reset_step, slot), table, (hidden, *halos, source, gates, w_hidden),
            [full, full] + [block] * 4, 2 * ROWS * 512 * 1024, scratch=(slots,),
        )
        halos = exchange(toward)
        update, partial = call(
            late_gates, table, (gates, mixed_h, state, w_hidden, w_cand), [wide, wide], 2 * ROWS * 512 * 1024
        )
        last, keep = t == 7, kept[t // 4]
        hidden, keep[slot], *toward = call(
            functools.partial(new_hidden, slot, t // 2, last), table,
            (hidden, state, *halos, source, update, partial, w_cand, keep[slot]),
            [full, full] + [block] * (0 if last else 4), 2 * ROWS * 512 * 1024,
            scratch=(slots, pltpu.VMEM((ROWS, HID), bf16)), aliases={11: 1},
        )
        if t in (3, 5, 7):
            snaps = {3: (0, 1, 2, 3), 5: (4, 5), 7: (6, 7)}[t]
            came += [
                [lax.ppermute(v, AXES, output_route(snaps, o)) for o, v in enumerate((
                    jnp.where(seq == 0, keep[0], keep[1]), jnp.where(seq == 0, keep[1], keep[0])))]
            ]
    first, second = [jnp.where(snap < 4, came[0][o], jnp.where(snap < 6, came[1][o], came[2][o])) for o in range(2)]
    flip = core == 0
    return jnp.stack([jnp.where(flip, first, second), jnp.where(flip, second, first)])[:, None]


def solution(mesh):
    return jax.shard_map(
        local,
        mesh=mesh,
        in_specs=(
            P(None, "tm", "graph", None),
            P("tm", "graph", None, None, None),
            P("tm", "graph", None),
            P("tm", "graph", None),
            P(),
            P(),
            P(),
            P(),
        ),
        out_specs=P(None, "tm", "graph", None),
        check_vma=False,
    )
```

```python
import functools

import jax
import jax.numpy as jnp
from jax import lax
from jax.experimental import pallas as pl
from jax.experimental.pallas import tpu as pltpu
from jax.sharding import PartitionSpec as P

OFFSETS = (-2, -1, 1, 2)
AXES = ("tm", "graph")
PARTS, BLK, HID, FEAT = 32, 128, 512, 128
ROWS = 2 * BLK
CYCLE = (
    (0, 0), (0, 1), (0, 2), (0, 3), (1, 3), (1, 2), (1, 1), (2, 1),
    (2, 2), (2, 3), (3, 3), (3, 2), (3, 1), (3, 0), (2, 0), (1, 0),
)
LADDER = ((0, 0), (0, 1), (1, 1), (1, 0))


def place(seq, pair, part):
    x, y = CYCLE[part // 2]
    plane_pair, core = LADDER[pair]
    z = 4 * seq + 2 * plane_pair + part % 2
    return (2 * y + core) * PARTS + x * 8 + z


EVERY = [(s, q, p) for s in range(2) for q in range(4) for p in range(PARTS)]


def exchange_route(offset, move=None):
    target = {None: lambda q: q, "swap": lambda q: q ^ 1, "next": lambda q: (q + 1) % 4}[move]
    return [(place(s, q, p), place(s, target(q), (p - offset) % PARTS)) for s, q, p in EVERY]


def input_route(other):
    return [((2 * q + (s ^ other)) * PARTS + p, place(s, q, p)) for s, q, p in EVERY]


def output_route(other):
    return [(b, a) for a, b in input_route(other)]


INPUT, SMALL = 1024, 1280
SEND, PAIR = 8, 12

VMEM = pl.BlockSpec(memory_space=pltpu.VMEM)
SMEM = pl.BlockSpec(memory_space=pltpu.SMEM)


def call(body, table, operands, outs, flops, scratch=(), aliases=None):
    shapes = [jax.ShapeDtypeStruct(shape, dtype) for shape, dtype in outs]
    size = sum(v.size * v.dtype.itemsize for v in (*operands, *shapes))
    return pl.pallas_call(
        body,
        out_shape=shapes,
        in_specs=[SMEM] + [VMEM] * len(operands),
        out_specs=[VMEM] * len(outs),
        scratch_shapes=list(scratch),
        input_output_aliases=aliases or {},
        compiler_params=pltpu.CompilerParams(vmem_limit_bytes=12 << 20),
        cost_estimate=pl.CostEstimate(flops=flops, bytes_accessed=size, transcendentals=0),
    )(table, *operands)


def dot(a, b):
    return jnp.dot(a, b, preferred_element_type=jnp.float32)


def graph_product(table, row, source, slots, out):
    for tile in range(2):
        at = tile * 4 * BLK
        weights = jnp.concatenate([source[at + k * BLK : at + (k + 1) * BLK, :] for k in range(4)], axis=1)
        picked = jnp.concatenate([slots[table[row, 4 * tile + k]] for k in range(4)], axis=0)
        out[tile * BLK : (tile + 1) * BLK, :] = dot(weights, picked).astype(jnp.bfloat16)


def fill(slots, own, halos):
    slots[0] = own[:BLK, :]
    slots[1] = own[BLK:, :]
    for i, halo in enumerate(halos):
        slots[2 + i] = halo[...]


def put_toward(table, row, own, toward):
    for i, out in enumerate(toward):
        start = pl.multiple_of(table[row, SEND + 3 - i] * BLK, BLK)
        out[...] = own[pl.ds(start, BLK), :]


def toward_inputs(table, even, odd, *outs):
    *toward, small = outs
    for slot, source in enumerate((even, odd)):
        for i, out in enumerate(toward):
            start = pl.multiple_of(INPUT + table[slot, SEND + 3 - i] * BLK, BLK)
            out[slot * BLK : (slot + 1) * BLK, :] = source[pl.ds(start, BLK), :]
    small[...] = even[SMALL:, :]


def mix_inputs(table, even, odd, h0, h1, h2, h3, mixed_even, mixed_odd, slots):
    for slot, (source, out) in enumerate(((even, mixed_even), (odd, mixed_odd))):
        slots[0] = source[INPUT : INPUT + BLK, :]
        slots[1] = source[INPUT + BLK : SMALL, :]
        for i, halo in enumerate((h0, h1, h2, h3)):
            slots[2 + i] = halo[slot * BLK : (slot + 1) * BLK, :]
        graph_product(table, slot, source, slots, out)


def input_gate(source, mixed, w_input, bias, cols):
    return (
        dot(source[INPUT:SMALL, :], w_input[0, :, cols])
        + dot(mixed[...], w_input[1, :, cols])
        + bias[:, cols]
    )


def first_step(table, source, mixed, w_input, bias, hidden, t0, t1, t2, t3):
    update = jax.nn.sigmoid(input_gate(source, mixed, w_input, bias, slice(0, HID)))
    candidate = jnp.tanh(input_gate(source, mixed, w_input, bias, slice(2 * HID, 3 * HID)))
    hidden[...] = ((1.0 - update) * candidate).astype(jnp.bfloat16)
    put_toward(table, 1, hidden, (t0, t1, t2, t3))


def early_gates(table, source, mixed, hidden, w_input, w_hidden, bias, gates):
    for column in range(3):
        cols = slice(column * HID, (column + 1) * HID)
        value = input_gate(source, mixed, w_input, bias, cols)
        if column < 2:
            value += dot(hidden[...], w_hidden[0, :, cols])
        gates[:, cols] = value


def reset_step(slot, table, hidden, h0, h1, h2, h3, source, gates, w_hidden, state, mixed, t0, t1, t2, t3, slots):
    fill(slots, hidden, (h0, h1, h2, h3))
    graph_product(table, slot, source, slots, mixed)
    reset = jax.nn.sigmoid(gates[:, HID : 2 * HID] + dot(mixed[...], w_hidden[1, :, HID:]))
    state[...] = (reset * hidden[...].astype(jnp.float32)).astype(jnp.bfloat16)
    put_toward(table, slot, state, (t0, t1, t2, t3))


def late_gates(table, gates, mixed, state, w_hidden, w_cand, update, partial):
    update[...] = jax.nn.sigmoid(gates[:, :HID] + dot(mixed[...], w_hidden[1, :, :HID]))
    partial[...] = gates[:, 2 * HID :] + dot(state[...], w_cand[0])


def new_hidden(slot, pair, last, table, hidden, state, h0, h1, h2, h3, source, update, partial, w_cand, kept_in, out, kept, *rest):
    *toward, slots, mixed = rest
    fill(slots, state, (h0, h1, h2, h3))
    graph_product(table, slot, source, slots, mixed)
    candidate = jnp.tanh(partial[...] + dot(mixed[...], w_cand[1]))
    gate = update[...]
    out[...] = (gate * hidden[...].astype(jnp.float32) + (1.0 - gate) * candidate).astype(jnp.bfloat16)
    if not last:
        put_toward(table, 1 + slot, out, toward)

    @pl.when(table[0, PAIR] == pair)
    def _():
        kept[...] = out[...]


def local(node_feats, adjacency, columns, send_list, w_input, w_hidden, w_cand, gate_bias):
    bf16, f32 = jnp.bfloat16, jnp.float32
    snap = lax.axis_index("tm")
    z, core = lax.axis_index("graph") % 8, snap % 2
    seq = z // 4
    bias = gate_bias[None, :]
    small = jnp.concatenate([columns.reshape(-1), send_list.reshape(-1), jnp.full((116,), snap // 2, jnp.int32)])
    small = jnp.broadcast_to(small.astype(bf16)[None], (16, 128))
    feats = node_feats[:, 0]
    mine = jnp.where(core == 0, feats[0], feats[1])
    others = jnp.where(core == 0, feats[1], feats[0])
    weights = adjacency.reshape(8 * BLK, BLK)
    got = [
        lax.ppermute(jnp.concatenate([weights, x, small], axis=0), AXES, input_route(other))
        for x, other in ((mine, 0), (others, 1))
    ]
    even = jnp.where(seq == 0, got[0], got[1])
    odd = jnp.where(seq == 0, got[1], got[0])
    block = ((BLK, HID), bf16)
    full = ((ROWS, HID), bf16)
    wide = ((ROWS, HID), f32)
    slots = pltpu.VMEM((6, BLK, HID), bf16)

    def integers(*rows):
        return jnp.concatenate([r[:1] for r in rows], axis=0).astype(jnp.int32)

    def exchange(blocks, move=None):
        return [lax.ppermute(b, AXES, exchange_route(o, move)) for b, o in zip(blocks, OFFSETS)]

    table = integers(even[SMALL:], odd[SMALL:])
    *toward, small = call(
        toward_inputs, table, (even, odd), [((2 * BLK, FEAT), bf16)] * 4 + [((16, 128), bf16)], 0
    )
    halos = exchange(toward)
    before = [(place(s, q, p), place(s, (q - 1) % 4, p)) for s, q, p in EVERY]
    following = lax.ppermute(small, AXES, before)
    mixes = call(
        mix_inputs, table, (even, odd, *halos), [((ROWS, FEAT), bf16)] * 2, 2 * 2 * ROWS * 512 * FEAT,
        scratch=(pltpu.VMEM((6, BLK, FEAT), bf16),),
    )
    hidden, *toward = call(
        first_step, table, (even, mixes[0], w_input, bias), [full] + [block] * 4, 2 * ROWS * 256 * 1024
    )
    table = integers(even[SMALL:], odd[SMALL:], following)
    kept = [hidden, hidden]
    sources = (even, odd)
    for t in range(1, 8):
        slot, move = t % 2, {2: "swap", 4: "next", 6: "swap"}.get(t)
        if move:
            hidden = lax.ppermute(hidden, AXES, exchange_route(0, move))
        halos = exchange(toward, move)
        (gates,) = call(
            early_gates, table, (sources[slot], mixes[slot], hidden, w_input, w_hidden, bias), [((ROWS, 3 * HID), f32)],
            2 * ROWS * (256 * 1536 + 512 * 1024),
        )
        state, mixed_h, *toward = call(
            functools.partial(reset_step, slot), table, (hidden, *halos, sources[slot], gates, w_hidden),
            [full, full] + [block] * 4, 2 * ROWS * 512 * 1024, scratch=(slots,),
        )
        halos = exchange(toward)
        update, partial = call(
            late_gates, table, (gates, mixed_h, state, w_hidden, w_cand), [wide, wide], 2 * ROWS * 512 * 1024
        )
        last = t == 7
        hidden, kept[slot], *toward = call(
            functools.partial(new_hidden, slot, t // 2, last), table,
            (hidden, state, *halos, sources[slot], update, partial, w_cand, kept[slot]),
            [full, full] + [block] * (0 if last else 4), 2 * ROWS * 512 * 1024,
            scratch=(slots, pltpu.VMEM((ROWS, HID), bf16)), aliases={11: 1},
        )
    first = lax.ppermute(jnp.where(seq == 0, kept[0], kept[1]), AXES, output_route(0))
    second = lax.ppermute(jnp.where(seq == 0, kept[1], kept[0]), AXES, output_route(1))
    flip = core == 0
    return jnp.stack([jnp.where(flip, first, second), jnp.where(flip, second, first)])[:, None]


def solution(mesh):
    return jax.shard_map(
        local,
        mesh=mesh,
        in_specs=(
            P(None, "tm", "graph", None),
            P("tm", "graph", None, None, None),
            P("tm", "graph", None),
            P("tm", "graph", None),
            P(),
            P(),
            P(),
            P(),
        ),
        out_specs=P(None, "tm", "graph", None),
        check_vma=False,
    )
```

```python
import functools

import jax
import jax.numpy as jnp
from jax import lax
from jax.experimental import pallas as pl
from jax.experimental.pallas import tpu as pltpu
from jax.sharding import PartitionSpec as P

OFFSETS = (-2, -1, 1, 2)
AXES = ("tm", "graph")
PARTS, BLK, HID, FEAT = 32, 128, 512, 128
ROWS = 2 * BLK
CYCLE = (
    (0, 0), (0, 1), (0, 2), (0, 3), (1, 3), (1, 2), (1, 1), (2, 1),
    (2, 2), (2, 3), (3, 3), (3, 2), (3, 1), (3, 0), (2, 0), (1, 0),
)
LADDER = ((0, 0), (0, 1), (1, 1), (1, 0))


def place(seq, pair, part):
    x, y = CYCLE[(part // 2 + 8 - pair // 2) % 16]
    plane_pair, core = LADDER[pair]
    z = 4 * seq + 2 * plane_pair + part % 2
    return (2 * y + core) * PARTS + x * 8 + z


EVERY = [(s, q, p) for s in range(2) for q in range(4) for p in range(PARTS)]


def exchange_route(offset, move=None):
    target = {None: lambda q: q, "swap": lambda q: q ^ 1, "next": lambda q: (q + 1) % 4}[move]
    return [(place(s, q, p), place(s, target(q), (p - offset) % PARTS)) for s, q, p in EVERY]


def input_route(other):
    return [((2 * q + (s ^ other)) * PARTS + p, place(s, q, p)) for s, q, p in EVERY]


def output_route(other):
    return [(b, a) for a, b in input_route(other)]


INPUT, SMALL = 1024, 1280
SEND, PAIR = 8, 12

VMEM = pl.BlockSpec(memory_space=pltpu.VMEM)
SMEM = pl.BlockSpec(memory_space=pltpu.SMEM)


def call(body, table, operands, outs, flops, scratch=(), aliases=None):
    shapes = [jax.ShapeDtypeStruct(shape, dtype) for shape, dtype in outs]
    size = sum(v.size * v.dtype.itemsize for v in (*operands, *shapes))
    return pl.pallas_call(
        body,
        out_shape=shapes,
        in_specs=[SMEM] + [VMEM] * len(operands),
        out_specs=[VMEM] * len(outs),
        scratch_shapes=list(scratch),
        input_output_aliases=aliases or {},
        compiler_params=pltpu.CompilerParams(vmem_limit_bytes=12 << 20),
        cost_estimate=pl.CostEstimate(flops=flops, bytes_accessed=size, transcendentals=0),
    )(table, *operands)


def dot(a, b):
    return jnp.dot(a, b, preferred_element_type=jnp.float32)


def graph_product(table, row, source, slots, out):
    for tile in range(2):
        at = tile * 4 * BLK
        weights = jnp.concatenate([source[at + k * BLK : at + (k + 1) * BLK, :] for k in range(4)], axis=1)
        picked = jnp.concatenate([slots[table[row, 4 * tile + k]] for k in range(4)], axis=0)
        out[tile * BLK : (tile + 1) * BLK, :] = dot(weights, picked).astype(jnp.bfloat16)


def fill(slots, own, halos):
    slots[0] = own[:BLK, :]
    slots[1] = own[BLK:, :]
    for i, halo in enumerate(halos):
        slots[2 + i] = halo[...]


def put_toward(table, row, own, toward):
    for i, out in enumerate(toward):
        start = pl.multiple_of(table[row, SEND + 3 - i] * BLK, BLK)
        out[...] = own[pl.ds(start, BLK), :]


def toward_inputs(table, even, odd, *outs):
    *toward, small = outs
    for slot, source in enumerate((even, odd)):
        for i, out in enumerate(toward):
            start = pl.multiple_of(INPUT + table[slot, SEND + 3 - i] * BLK, BLK)
            out[slot * BLK : (slot + 1) * BLK, :] = source[pl.ds(start, BLK), :]
    small[...] = even[SMALL:, :]


def mix_inputs(table, even, odd, h0, h1, h2, h3, mixed_even, mixed_odd, slots):
    for slot, (source, out) in enumerate(((even, mixed_even), (odd, mixed_odd))):
        slots[0] = source[INPUT : INPUT + BLK, :]
        slots[1] = source[INPUT + BLK : SMALL, :]
        for i, halo in enumerate((h0, h1, h2, h3)):
            slots[2 + i] = halo[slot * BLK : (slot + 1) * BLK, :]
        graph_product(table, slot, source, slots, out)


def input_gate(source, mixed, w_input, bias, cols):
    return (
        dot(source[INPUT:SMALL, :], w_input[0, :, cols])
        + dot(mixed[...], w_input[1, :, cols])
        + bias[:, cols]
    )


def first_step(table, source, mixed, w_input, bias, hidden, t0, t1, t2, t3):
    update = jax.nn.sigmoid(input_gate(source, mixed, w_input, bias, slice(0, HID)))
    candidate = jnp.tanh(input_gate(source, mixed, w_input, bias, slice(2 * HID, 3 * HID)))
    hidden[...] = ((1.0 - update) * candidate).astype(jnp.bfloat16)
    put_toward(table, 1, hidden, (t0, t1, t2, t3))


def early_gates(table, source, mixed, hidden, w_input, w_hidden, bias, gates):
    for column in range(3):
        cols = slice(column * HID, (column + 1) * HID)
        value = input_gate(source, mixed, w_input, bias, cols)
        if column < 2:
            value += dot(hidden[...], w_hidden[0, :, cols])
        gates[:, cols] = value


def reset_step(slot, table, hidden, h0, h1, h2, h3, source, gates, w_hidden, state, mixed, t0, t1, t2, t3, slots):
    fill(slots, hidden, (h0, h1, h2, h3))
    graph_product(table, slot, source, slots, mixed)
    reset = jax.nn.sigmoid(gates[:, HID : 2 * HID] + dot(mixed[...], w_hidden[1, :, HID:]))
    state[...] = (reset * hidden[...].astype(jnp.float32)).astype(jnp.bfloat16)
    put_toward(table, slot, state, (t0, t1, t2, t3))


def late_gates(table, gates, mixed, state, w_hidden, w_cand, update, partial):
    update[...] = jax.nn.sigmoid(gates[:, :HID] + dot(mixed[...], w_hidden[1, :, :HID]))
    partial[...] = gates[:, 2 * HID :] + dot(state[...], w_cand[0])


def new_hidden(slot, pair, last, table, hidden, state, h0, h1, h2, h3, source, update, partial, w_cand, kept_in, out, kept, *rest):
    *toward, slots, mixed = rest
    fill(slots, state, (h0, h1, h2, h3))
    graph_product(table, slot, source, slots, mixed)
    candidate = jnp.tanh(partial[...] + dot(mixed[...], w_cand[1]))
    gate = update[...]
    out[...] = (gate * hidden[...].astype(jnp.float32) + (1.0 - gate) * candidate).astype(jnp.bfloat16)
    if not last:
        put_toward(table, 1 + slot, out, toward)

    @pl.when(table[0, PAIR] == pair)
    def _():
        kept[...] = out[...]


def local(node_feats, adjacency, columns, send_list, w_input, w_hidden, w_cand, gate_bias):
    bf16, f32 = jnp.bfloat16, jnp.float32
    snap = lax.axis_index("tm")
    z, core = lax.axis_index("graph") % 8, snap % 2
    seq = z // 4
    bias = gate_bias[None, :]
    small = jnp.concatenate([columns.reshape(-1), send_list.reshape(-1), jnp.full((116,), snap // 2, jnp.int32)])
    small = jnp.broadcast_to(small.astype(bf16)[None], (16, 128))
    feats = node_feats[:, 0]
    mine = jnp.where(core == 0, feats[0], feats[1])
    others = jnp.where(core == 0, feats[1], feats[0])
    weights = adjacency.reshape(8 * BLK, BLK)
    got = [
        lax.ppermute(jnp.concatenate([weights, x, small], axis=0), AXES, input_route(other))
        for x, other in ((mine, 0), (others, 1))
    ]
    even = jnp.where(seq == 0, got[0], got[1])
    odd = jnp.where(seq == 0, got[1], got[0])
    block = ((BLK, HID), bf16)
    full = ((ROWS, HID), bf16)
    wide = ((ROWS, HID), f32)
    slots = pltpu.VMEM((6, BLK, HID), bf16)

    def integers(*rows):
        return jnp.concatenate([r[:1] for r in rows], axis=0).astype(jnp.int32)

    def exchange(blocks, move=None):
        return [lax.ppermute(b, AXES, exchange_route(o, move)) for b, o in zip(blocks, OFFSETS)]

    table = integers(even[SMALL:], odd[SMALL:])
    *toward, small = call(
        toward_inputs, table, (even, odd), [((2 * BLK, FEAT), bf16)] * 4 + [((16, 128), bf16)], 0
    )
    halos = exchange(toward)
    before = [(place(s, q, p), place(s, (q - 1) % 4, p)) for s, q, p in EVERY]
    following = lax.ppermute(small, AXES, before)
    mixes = call(
        mix_inputs, table, (even, odd, *halos), [((ROWS, FEAT), bf16)] * 2, 2 * 2 * ROWS * 512 * FEAT,
        scratch=(pltpu.VMEM((6, BLK, FEAT), bf16),),
    )
    hidden, *toward = call(
        first_step, table, (even, mixes[0], w_input, bias), [full] + [block] * 4, 2 * ROWS * 256 * 1024
    )
    table = integers(even[SMALL:], odd[SMALL:], following)
    kept = [hidden, hidden]
    sources = (even, odd)
    for t in range(1, 8):
        slot, move = t % 2, {2: "swap", 4: "next", 6: "swap"}.get(t)
        if move:
            hidden = lax.ppermute(hidden, AXES, exchange_route(0, move))
        halos = exchange(toward, move)
        (gates,) = call(
            early_gates, table, (sources[slot], mixes[slot], hidden, w_input, w_hidden, bias), [((ROWS, 3 * HID), f32)],
            2 * ROWS * (256 * 1536 + 512 * 1024),
        )
        state, mixed_h, *toward = call(
            functools.partial(reset_step, slot), table, (hidden, *halos, sources[slot], gates, w_hidden),
            [full, full] + [block] * 4, 2 * ROWS * 512 * 1024, scratch=(slots,),
        )
        halos = exchange(toward)
        update, partial = call(
            late_gates, table, (gates, mixed_h, state, w_hidden, w_cand), [wide, wide], 2 * ROWS * 512 * 1024
        )
        last = t == 7
        hidden, kept[slot], *toward = call(
            functools.partial(new_hidden, slot, t // 2, last), table,
            (hidden, state, *halos, sources[slot], update, partial, w_cand, kept[slot]),
            [full, full] + [block] * (0 if last else 4), 2 * ROWS * 512 * 1024,
            scratch=(slots, pltpu.VMEM((ROWS, HID), bf16)), aliases={11: 1},
        )
    first = lax.ppermute(jnp.where(seq == 0, kept[0], kept[1]), AXES, output_route(0))
    second = lax.ppermute(jnp.where(seq == 0, kept[1], kept[0]), AXES, output_route(1))
    flip = core == 0
    return jnp.stack([jnp.where(flip, first, second), jnp.where(flip, second, first)])[:, None]


def solution(mesh):
    return jax.shard_map(
        local,
        mesh=mesh,
        in_specs=(
            P(None, "tm", "graph", None),
            P("tm", "graph", None, None, None),
            P("tm", "graph", None),
            P("tm", "graph", None),
            P(),
            P(),
            P(),
            P(),
        ),
        out_specs=P(None, "tm", "graph", None),
        check_vma=False,
    )
```

```python
import functools

import jax
import jax.numpy as jnp
from jax import lax
from jax.experimental import pallas as pl
from jax.experimental.pallas import tpu as pltpu
from jax.sharding import PartitionSpec as P

OFFSETS = (-2, -1, 1, 2)
ORDER = (1, 2, 0, 3)
AXES = ("tm", "graph")
PARTS, BLK, HID, FEAT = 32, 128, 512, 128
ROWS = 2 * BLK
CYCLE = (
    (0, 0), (0, 1), (0, 2), (0, 3), (1, 3), (1, 2), (1, 1), (2, 1),
    (2, 2), (2, 3), (3, 3), (3, 2), (3, 1), (3, 0), (2, 0), (1, 0),
)
LADDER = ((0, 0), (0, 1), (1, 1), (1, 0))


def place(seq, pair, part):
    x, y = CYCLE[part // 2]
    plane_pair, core = LADDER[pair]
    z = 4 * seq + 2 * plane_pair + part % 2
    return (2 * y + core) * PARTS + x * 8 + z


EVERY = [(s, q, p) for s in range(2) for q in range(4) for p in range(PARTS)]


def exchange_route(offset, move=None):
    target = {None: lambda q: q, "swap": lambda q: q ^ 1, "next": lambda q: (q + 1) % 4}[move]
    return [(place(s, q, p), place(s, target(q), (p - offset) % PARTS)) for s, q, p in EVERY]


def input_route(other):
    return [((2 * q + (s ^ other)) * PARTS + p, place(s, q, p)) for s, q, p in EVERY]


def output_route(other):
    return [(b, a) for a, b in input_route(other)]


INPUT, SMALL = 1024, 1280
SEND, PAIR = 8, 12

VMEM = pl.BlockSpec(memory_space=pltpu.VMEM)
SMEM = pl.BlockSpec(memory_space=pltpu.SMEM)


def call(body, table, operands, outs, flops, scratch=(), aliases=None):
    shapes = [jax.ShapeDtypeStruct(shape, dtype) for shape, dtype in outs]
    size = sum(v.size * v.dtype.itemsize for v in (*operands, *shapes))
    return pl.pallas_call(
        body,
        out_shape=shapes,
        in_specs=[SMEM] + [VMEM] * len(operands),
        out_specs=[VMEM] * len(outs),
        scratch_shapes=list(scratch),
        input_output_aliases=aliases or {},
        compiler_params=pltpu.CompilerParams(vmem_limit_bytes=12 << 20),
        cost_estimate=pl.CostEstimate(flops=flops, bytes_accessed=size, transcendentals=0),
    )(table, *operands)


def dot(a, b):
    return jnp.dot(a, b, preferred_element_type=jnp.float32)


def graph_product(table, row, source, slots, out):
    for tile in range(2):
        at = tile * 4 * BLK
        weights = jnp.concatenate([source[at + k * BLK : at + (k + 1) * BLK, :] for k in range(4)], axis=1)
        picked = jnp.concatenate([slots[table[row, 4 * tile + k]] for k in range(4)], axis=0)
        out[tile * BLK : (tile + 1) * BLK, :] = dot(weights, picked).astype(jnp.bfloat16)


def fill(slots, own, halos):
    slots[0] = own[:BLK, :]
    slots[1] = own[BLK:, :]
    for i, halo in zip(ORDER, halos):
        slots[2 + i] = halo[...]


def put_toward(table, row, own, toward):
    for i, out in enumerate(toward):
        start = pl.multiple_of(table[row, SEND + 3 - i] * BLK, BLK)
        out[...] = own[pl.ds(start, BLK), :]


def toward_inputs(table, even, odd, *outs):
    *toward, small = outs
    for slot, source in enumerate((even, odd)):
        for i, out in enumerate(toward):
            start = pl.multiple_of(INPUT + table[slot, SEND + 3 - i] * BLK, BLK)
            out[slot * BLK : (slot + 1) * BLK, :] = source[pl.ds(start, BLK), :]
    small[...] = even[SMALL:, :]


def mix_inputs(table, even, odd, h0, h1, h2, h3, mixed_even, mixed_odd, slots):
    for slot, (source, out) in enumerate(((even, mixed_even), (odd, mixed_odd))):
        slots[0] = source[INPUT : INPUT + BLK, :]
        slots[1] = source[INPUT + BLK : SMALL, :]
        for i, halo in zip(ORDER, (h0, h1, h2, h3)):
            slots[2 + i] = halo[slot * BLK : (slot + 1) * BLK, :]
        graph_product(table, slot, source, slots, out)


def input_gate(source, mixed, w_input, bias, cols):
    return (
        dot(source[INPUT:SMALL, :], w_input[0, :, cols])
        + dot(mixed[...], w_input[1, :, cols])
        + bias[:, cols]
    )


def first_step(table, source, mixed, w_input, bias, hidden, t0, t1, t2, t3):
    update = jax.nn.sigmoid(input_gate(source, mixed, w_input, bias, slice(0, HID)))
    candidate = jnp.tanh(input_gate(source, mixed, w_input, bias, slice(2 * HID, 3 * HID)))
    hidden[...] = ((1.0 - update) * candidate).astype(jnp.bfloat16)
    put_toward(table, 1, hidden, (t0, t1, t2, t3))


def early_gates(table, source, mixed, hidden, w_input, w_hidden, bias, gates):
    for column in range(3):
        cols = slice(column * HID, (column + 1) * HID)
        value = input_gate(source, mixed, w_input, bias, cols)
        if column < 2:
            value += dot(hidden[...], w_hidden[0, :, cols])
        gates[:, cols] = value


def reset_step(slot, table, hidden, h0, h1, h2, h3, source, gates, w_hidden, state, mixed, t0, t1, t2, t3, slots):
    fill(slots, hidden, (h0, h1, h2, h3))
    graph_product(table, slot, source, slots, mixed)
    reset = jax.nn.sigmoid(gates[:, HID : 2 * HID] + dot(mixed[...], w_hidden[1, :, HID:]))
    state[...] = (reset * hidden[...].astype(jnp.float32)).astype(jnp.bfloat16)
    put_toward(table, slot, state, (t0, t1, t2, t3))


def late_gates(table, gates, mixed, state, w_hidden, w_cand, update, partial):
    update[...] = jax.nn.sigmoid(gates[:, :HID] + dot(mixed[...], w_hidden[1, :, :HID]))
    partial[...] = gates[:, 2 * HID :] + dot(state[...], w_cand[0])


def new_hidden(slot, pair, last, table, hidden, state, h0, h1, h2, h3, source, update, partial, w_cand, kept_in, out, kept, *rest):
    *toward, slots, mixed = rest
    fill(slots, state, (h0, h1, h2, h3))
    graph_product(table, slot, source, slots, mixed)
    candidate = jnp.tanh(partial[...] + dot(mixed[...], w_cand[1]))
    gate = update[...]
    out[...] = (gate * hidden[...].astype(jnp.float32) + (1.0 - gate) * candidate).astype(jnp.bfloat16)
    if not last:
        put_toward(table, 1 + slot, out, toward)

    @pl.when(table[0, PAIR] == pair)
    def _():
        kept[...] = out[...]


def local(node_feats, adjacency, columns, send_list, w_input, w_hidden, w_cand, gate_bias):
    bf16, f32 = jnp.bfloat16, jnp.float32
    snap = lax.axis_index("tm")
    z, core = lax.axis_index("graph") % 8, snap % 2
    seq = z // 4
    bias = gate_bias[None, :]
    small = jnp.concatenate([columns.reshape(-1), send_list.reshape(-1), jnp.full((116,), snap // 2, jnp.int32)])
    small = jnp.broadcast_to(small.astype(bf16)[None], (16, 128))
    feats = node_feats[:, 0]
    mine = jnp.where(core == 0, feats[0], feats[1])
    others = jnp.where(core == 0, feats[1], feats[0])
    weights = adjacency.reshape(8 * BLK, BLK)
    got = [
        lax.ppermute(jnp.concatenate([weights, x, small], axis=0), AXES, input_route(other))
        for x, other in ((mine, 0), (others, 1))
    ]
    even = jnp.where(seq == 0, got[0], got[1])
    odd = jnp.where(seq == 0, got[1], got[0])
    block = ((BLK, HID), bf16)
    full = ((ROWS, HID), bf16)
    wide = ((ROWS, HID), f32)
    slots = pltpu.VMEM((6, BLK, HID), bf16)

    def integers(*rows):
        return jnp.concatenate([r[:1] for r in rows], axis=0).astype(jnp.int32)

    def exchange(blocks, move=None):
        return [lax.ppermute(blocks[i], AXES, exchange_route(OFFSETS[i], move)) for i in ORDER]

    table = integers(even[SMALL:], odd[SMALL:])
    *toward, small = call(
        toward_inputs, table, (even, odd), [((2 * BLK, FEAT), bf16)] * 4 + [((16, 128), bf16)], 0
    )
    halos = exchange(toward)
    before = [(place(s, q, p), place(s, (q - 1) % 4, p)) for s, q, p in EVERY]
    following = lax.ppermute(small, AXES, before)
    mixes = call(
        mix_inputs, table, (even, odd, *halos), [((ROWS, FEAT), bf16)] * 2, 2 * 2 * ROWS * 512 * FEAT,
        scratch=(pltpu.VMEM((6, BLK, FEAT), bf16),),
    )
    hidden, *toward = call(
        first_step, table, (even, mixes[0], w_input, bias), [full] + [block] * 4, 2 * ROWS * 256 * 1024
    )
    table = integers(even[SMALL:], odd[SMALL:], following)
    kept = [hidden, hidden]
    sources = (even, odd)
    for t in range(1, 8):
        slot, move = t % 2, {2: "swap", 4: "next", 6: "swap"}.get(t)
        if move:
            hidden = lax.ppermute(hidden, AXES, exchange_route(0, move))
        halos = exchange(toward, move)
        (gates,) = call(
            early_gates, table, (sources[slot], mixes[slot], hidden, w_input, w_hidden, bias), [((ROWS, 3 * HID), f32)],
            2 * ROWS * (256 * 1536 + 512 * 1024),
        )
        state, mixed_h, *toward = call(
            functools.partial(reset_step, slot), table, (hidden, *halos, sources[slot], gates, w_hidden),
            [full, full] + [block] * 4, 2 * ROWS * 512 * 1024, scratch=(slots,),
        )
        halos = exchange(toward)
        update, partial = call(
            late_gates, table, (gates, mixed_h, state, w_hidden, w_cand), [wide, wide], 2 * ROWS * 512 * 1024
        )
        last = t == 7
        hidden, kept[slot], *toward = call(
            functools.partial(new_hidden, slot, t // 2, last), table,
            (hidden, state, *halos, sources[slot], update, partial, w_cand, kept[slot]),
            [full, full] + [block] * (0 if last else 4), 2 * ROWS * 512 * 1024,
            scratch=(slots, pltpu.VMEM((ROWS, HID), bf16)), aliases={11: 1},
        )
    first = lax.ppermute(jnp.where(seq == 0, kept[0], kept[1]), AXES, output_route(0))
    second = lax.ppermute(jnp.where(seq == 0, kept[1], kept[0]), AXES, output_route(1))
    flip = core == 0
    return jnp.stack([jnp.where(flip, first, second), jnp.where(flip, second, first)])[:, None]


def solution(mesh):
    return jax.shard_map(
        local,
        mesh=mesh,
        in_specs=(
            P(None, "tm", "graph", None),
            P("tm", "graph", None, None, None),
            P("tm", "graph", None),
            P("tm", "graph", None),
            P(),
            P(),
            P(),
            P(),
        ),
        out_specs=P(None, "tm", "graph", None),
        check_vma=False,
    )
```

```python
import functools

import jax
import jax.numpy as jnp
from jax import lax
from jax.experimental import pallas as pl
from jax.experimental.pallas import tpu as pltpu
from jax.sharding import PartitionSpec as P

OFFSETS = (-2, -1, 1, 2)
ORDER = (1, 2, 0, 3)
AXES = ("tm", "graph")
PARTS, BLK, HID, FEAT = 32, 128, 512, 128
ROWS = 2 * BLK
CYCLE = (
    (0, 0), (0, 1), (0, 2), (0, 3), (1, 3), (1, 2), (1, 1), (2, 1),
    (2, 2), (2, 3), (3, 3), (3, 2), (3, 1), (3, 0), (2, 0), (1, 0),
)
LADDER = ((0, 0), (0, 1), (1, 1), (1, 0))


def place(seq, pair, part):
    x, y = CYCLE[part // 2]
    plane_pair, core = LADDER[pair]
    z = 4 * seq + 2 * plane_pair + part % 2
    return (2 * y + core) * PARTS + x * 8 + z


EVERY = [(s, q, p) for s in range(2) for q in range(4) for p in range(PARTS)]


def exchange_route(offset, move=None):
    target = {None: lambda q: q, "swap": lambda q: q ^ 1, "next": lambda q: (q + 1) % 4}[move]
    return [(place(s, q, p), place(s, target(q), (p - offset) % PARTS)) for s, q, p in EVERY]


def input_route(other):
    return [((2 * q + (s ^ other)) * PARTS + p, place(s, q, p)) for s, q, p in EVERY]


def output_route(other):
    return [(b, a) for a, b in input_route(other)]


INPUT, SMALL = 1024, 1280
SEND, PAIR = 8, 12

VMEM = pl.BlockSpec(memory_space=pltpu.VMEM)
SMEM = pl.BlockSpec(memory_space=pltpu.SMEM)


def call(body, table, operands, outs, flops, scratch=(), aliases=None):
    shapes = [jax.ShapeDtypeStruct(shape, dtype) for shape, dtype in outs]
    size = sum(v.size * v.dtype.itemsize for v in (*operands, *shapes))
    return pl.pallas_call(
        body,
        out_shape=shapes,
        in_specs=[SMEM] + [VMEM] * len(operands),
        out_specs=[VMEM] * len(outs),
        scratch_shapes=list(scratch),
        input_output_aliases=aliases or {},
        compiler_params=pltpu.CompilerParams(vmem_limit_bytes=12 << 20),
        cost_estimate=pl.CostEstimate(flops=flops, bytes_accessed=size, transcendentals=0),
    )(table, *operands)


def dot(a, b):
    return jnp.dot(a, b, preferred_element_type=jnp.float32)


def graph_product(table, row, source, slots, out):
    for tile in range(2):
        at = tile * 4 * BLK
        weights = jnp.concatenate([source[at + k * BLK : at + (k + 1) * BLK, :] for k in range(4)], axis=1)
        picked = jnp.concatenate([slots[table[row, 4 * tile + k]] for k in range(4)], axis=0)
        out[tile * BLK : (tile + 1) * BLK, :] = dot(weights, picked).astype(jnp.bfloat16)


def fill(slots, own, halos):
    slots[0] = own[:BLK, :]
    slots[1] = own[BLK:, :]
    for i, halo in zip(ORDER, halos):
        slots[2 + i] = halo[...]


def put_toward(table, row, own, toward):
    for i, out in enumerate(toward):
        start = pl.multiple_of(table[row, SEND + 3 - i] * BLK, BLK)
        out[...] = own[pl.ds(start, BLK), :]


def pack_inputs(columns, sends, snap, weights, feats, first, second):
    core = snap[0] & 1
    lanes = lax.broadcasted_iota(jnp.int32, (16, 128), 1)
    small = jnp.full((16, 128), snap[0] >> 1, jnp.int32)
    for k in range(8):
        small = jnp.where(lanes == k, columns[k], small)
    for k in range(4):
        small = jnp.where(lanes == SEND + k, sends[k], small)
    small = small.astype(jnp.float32).astype(jnp.bfloat16)
    for out, which in ((first, core), (second, 1 - core)):
        out[:INPUT, :] = weights[...]
        out[INPUT:SMALL, :] = feats[which]
        out[SMALL:, :] = small


def toward_inputs(table, even, odd, *outs):
    *toward, small = outs
    for slot, source in enumerate((even, odd)):
        for i, out in enumerate(toward):
            start = pl.multiple_of(INPUT + table[slot, SEND + 3 - i] * BLK, BLK)
            out[slot * BLK : (slot + 1) * BLK, :] = source[pl.ds(start, BLK), :]
    small[...] = even[SMALL:, :]


def mix_inputs(table, even, odd, h0, h1, h2, h3, mixed_even, mixed_odd, slots):
    for slot, (source, out) in enumerate(((even, mixed_even), (odd, mixed_odd))):
        slots[0] = source[INPUT : INPUT + BLK, :]
        slots[1] = source[INPUT + BLK : SMALL, :]
        for i, halo in zip(ORDER, (h0, h1, h2, h3)):
            slots[2 + i] = halo[slot * BLK : (slot + 1) * BLK, :]
        graph_product(table, slot, source, slots, out)


def input_gate(source, mixed, w_input, bias, cols):
    return (
        dot(source[INPUT:SMALL, :], w_input[0, :, cols])
        + dot(mixed[...], w_input[1, :, cols])
        + bias[:, cols]
    )


def first_step(table, source, mixed, w_input, bias, hidden, t0, t1, t2, t3):
    update = jax.nn.sigmoid(input_gate(source, mixed, w_input, bias, slice(0, HID)))
    candidate = jnp.tanh(input_gate(source, mixed, w_input, bias, slice(2 * HID, 3 * HID)))
    hidden[...] = ((1.0 - update) * candidate).astype(jnp.bfloat16)
    put_toward(table, 1, hidden, (t0, t1, t2, t3))


def early_gates(table, source, mixed, hidden, w_input, w_hidden, bias, gates):
    for column in range(3):
        cols = slice(column * HID, (column + 1) * HID)
        value = input_gate(source, mixed, w_input, bias, cols)
        if column < 2:
            value += dot(hidden[...], w_hidden[0, :, cols])
        gates[:, cols] = value


def reset_step(slot, table, hidden, h0, h1, h2, h3, source, gates, w_hidden, state, mixed, t0, t1, t2, t3, slots):
    fill(slots, hidden, (h0, h1, h2, h3))
    graph_product(table, slot, source, slots, mixed)
    reset = jax.nn.sigmoid(gates[:, HID : 2 * HID] + dot(mixed[...], w_hidden[1, :, HID:]))
    state[...] = (reset * hidden[...].astype(jnp.float32)).astype(jnp.bfloat16)
    put_toward(table, slot, state, (t0, t1, t2, t3))


def late_gates(table, gates, mixed, state, w_hidden, w_cand, update, partial):
    update[...] = jax.nn.sigmoid(gates[:, :HID] + dot(mixed[...], w_hidden[1, :, :HID]))
    partial[...] = gates[:, 2 * HID :] + dot(state[...], w_cand[0])


def new_hidden(slot, pair, last, table, hidden, state, h0, h1, h2, h3, source, update, partial, w_cand, kept_in, out, kept, *rest):
    *toward, slots, mixed = rest
    fill(slots, state, (h0, h1, h2, h3))
    graph_product(table, slot, source, slots, mixed)
    candidate = jnp.tanh(partial[...] + dot(mixed[...], w_cand[1]))
    gate = update[...]
    out[...] = (gate * hidden[...].astype(jnp.float32) + (1.0 - gate) * candidate).astype(jnp.bfloat16)
    if not last:
        put_toward(table, 1 + slot, out, toward)

    @pl.when(table[0, PAIR] == pair)
    def _():
        kept[...] = out[...]


def local(node_feats, adjacency, columns, send_list, w_input, w_hidden, w_cand, gate_bias):
    bf16, f32 = jnp.bfloat16, jnp.float32
    snap = lax.axis_index("tm")
    z, core = lax.axis_index("graph") % 8, snap % 2
    seq = z // 4
    bias = gate_bias[None, :]
    packed = pl.pallas_call(
        pack_inputs,
        out_shape=[jax.ShapeDtypeStruct((SMALL + 16, BLK), bf16)] * 2,
        in_specs=[SMEM] * 3 + [VMEM] * 2,
        out_specs=[VMEM] * 2,
        compiler_params=pltpu.CompilerParams(vmem_limit_bytes=12 << 20),
    )(columns.reshape(-1), send_list.reshape(-1), snap.reshape(1), adjacency.reshape(8 * BLK, BLK), node_feats[:, 0])
    got = [lax.ppermute(v, AXES, input_route(other)) for other, v in enumerate(packed)]
    even = jnp.where(seq == 0, got[0], got[1])
    odd = jnp.where(seq == 0, got[1], got[0])
    block = ((BLK, HID), bf16)
    full = ((ROWS, HID), bf16)
    wide = ((ROWS, HID), f32)
    slots = pltpu.VMEM((6, BLK, HID), bf16)

    def integers(*rows):
        return jnp.concatenate([r[:1] for r in rows], axis=0).astype(jnp.int32)

    def exchange(blocks, move=None):
        return [lax.ppermute(blocks[i], AXES, exchange_route(OFFSETS[i], move)) for i in ORDER]

    table = integers(even[SMALL:], odd[SMALL:])
    *toward, small = call(
        toward_inputs, table, (even, odd), [((2 * BLK, FEAT), bf16)] * 4 + [((16, 128), bf16)], 0
    )
    halos = exchange(toward)
    mixes = call(
        mix_inputs, table, (even, odd, *halos), [((ROWS, FEAT), bf16)] * 2, 2 * 2 * ROWS * 512 * FEAT,
        scratch=(pltpu.VMEM((6, BLK, FEAT), bf16),),
    )
    hidden, *toward = call(
        first_step, table, (even, mixes[0], w_input, bias), [full] + [block] * 4, 2 * ROWS * 256 * 1024
    )
    before = [(place(s, q, p), place(s, (q - 1) % 4, p)) for s, q, p in EVERY]
    small, hidden = lax.optimization_barrier((small, hidden))
    following = lax.ppermute(small, AXES, before)
    later_table = integers(even[SMALL:], odd[SMALL:], following)
    kept = [hidden, hidden]
    sources = (even, odd)
    for t in range(1, 8):
        slot, move = t % 2, {2: "swap", 4: "next", 6: "swap"}.get(t)
        if move:
            hidden = lax.ppermute(hidden, AXES, exchange_route(0, move))
        halos = exchange(toward, move)
        (gates,) = call(
            early_gates, table, (sources[slot], mixes[slot], hidden, w_input, w_hidden, bias), [((ROWS, 3 * HID), f32)],
            2 * ROWS * (256 * 1536 + 512 * 1024),
        )
        state, mixed_h, *toward = call(
            functools.partial(reset_step, slot), table, (hidden, *halos, sources[slot], gates, w_hidden),
            [full, full] + [block] * 4, 2 * ROWS * 512 * 1024, scratch=(slots,),
        )
        halos = exchange(toward)
        update, partial = call(
            late_gates, table, (gates, mixed_h, state, w_hidden, w_cand), [wide, wide], 2 * ROWS * 512 * 1024
        )
        last = t == 7
        hidden, kept[slot], *toward = call(
            functools.partial(new_hidden, slot, t // 2, last), later_table,
            (hidden, state, *halos, sources[slot], update, partial, w_cand, kept[slot]),
            [full, full] + [block] * (0 if last else 4), 2 * ROWS * 512 * 1024,
            scratch=(slots, pltpu.VMEM((ROWS, HID), bf16)), aliases={11: 1},
        )
    first = lax.ppermute(jnp.where(seq == 0, kept[0], kept[1]), AXES, output_route(0))
    second = lax.ppermute(jnp.where(seq == 0, kept[1], kept[0]), AXES, output_route(1))
    flip = core == 0
    return jnp.stack([jnp.where(flip, first, second), jnp.where(flip, second, first)])[:, None]


def solution(mesh):
    return jax.shard_map(
        local,
        mesh=mesh,
        in_specs=(
            P(None, "tm", "graph", None),
            P("tm", "graph", None, None, None),
            P("tm", "graph", None),
            P("tm", "graph", None),
            P(),
            P(),
            P(),
            P(),
        ),
        out_specs=P(None, "tm", "graph", None),
        check_vma=False,
    )
```

```python
import functools

import jax
import jax.numpy as jnp
from jax import lax
from jax.experimental import pallas as pl
from jax.experimental.pallas import tpu as pltpu
from jax.sharding import PartitionSpec as P

OFFSETS = (-2, -1, 1, 2)
ORDER = (1, 2, 0, 3)
AXES = ("tm", "graph")
PARTS, BLK, HID, FEAT = 32, 128, 512, 128
ROWS = 2 * BLK
CYCLE = (
    (0, 0), (0, 1), (0, 2), (0, 3), (1, 3), (1, 2), (1, 1), (2, 1),
    (2, 2), (2, 3), (3, 3), (3, 2), (3, 1), (3, 0), (2, 0), (1, 0),
)
LADDER = ((0, 0), (0, 1), (1, 1), (1, 0))


def place(seq, pair, part):
    x, y = CYCLE[part // 2]
    plane_pair, core = LADDER[pair]
    z = 4 * seq + 2 * plane_pair + part % 2
    return (2 * y + core) * PARTS + x * 8 + z


EVERY = [(s, q, p) for s in range(2) for q in range(4) for p in range(PARTS)]


def exchange_route(offset, move=None):
    target = {None: lambda q: q, "swap": lambda q: q ^ 1, "next": lambda q: (q + 1) % 4}[move]
    return [(place(s, q, p), place(s, target(q), (p - offset) % PARTS)) for s, q, p in EVERY]


def input_route(other):
    return [((2 * q + (s ^ other)) * PARTS + p, place(s, q, p)) for s, q, p in EVERY]


def output_route(other):
    return [(b, a) for a, b in input_route(other)]


INPUT, SMALL = 1024, 1280
SEND, PAIR = 8, 12

VMEM = pl.BlockSpec(memory_space=pltpu.VMEM)
SMEM = pl.BlockSpec(memory_space=pltpu.SMEM)


def call(body, table, operands, outs, flops, scratch=(), aliases=None):
    shapes = [jax.ShapeDtypeStruct(shape, dtype) for shape, dtype in outs]
    size = sum(v.size * v.dtype.itemsize for v in (*operands, *shapes))
    return pl.pallas_call(
        body,
        out_shape=shapes,
        in_specs=[SMEM] + [VMEM] * len(operands),
        out_specs=[VMEM] * len(outs),
        scratch_shapes=list(scratch),
        input_output_aliases=aliases or {},
        compiler_params=pltpu.CompilerParams(vmem_limit_bytes=12 << 20),
        cost_estimate=pl.CostEstimate(flops=flops, bytes_accessed=size, transcendentals=0),
    )(table, *operands)


def dot(a, b):
    return jnp.dot(a, b, preferred_element_type=jnp.float32)


def graph_product(table, row, source, slots, out):
    for tile in range(2):
        at = tile * 4 * BLK
        weights = jnp.concatenate([source[at + k * BLK : at + (k + 1) * BLK, :] for k in range(4)], axis=1)
        picked = jnp.concatenate([slots[table[row, 4 * tile + k]] for k in range(4)], axis=0)
        out[tile * BLK : (tile + 1) * BLK, :] = dot(weights, picked).astype(jnp.bfloat16)


def fill(slots, own, halos):
    slots[0] = own[:BLK, :]
    slots[1] = own[BLK:, :]
    for i, halo in zip(ORDER, halos):
        slots[2 + i] = halo[...]


def put_toward(table, row, own, toward):
    for i, out in enumerate(toward):
        start = pl.multiple_of(table[row, SEND + 3 - i] * BLK, BLK)
        out[...] = own[pl.ds(start, BLK), :]


def pack_inputs(columns, sends, snap, weights, feats, first, second):
    core = snap[0] & 1
    lanes = lax.broadcasted_iota(jnp.int32, (16, 128), 1)
    small = jnp.full((16, 128), snap[0] >> 1, jnp.int32)
    for k in range(8):
        small = jnp.where(lanes == k, columns[k], small)
    for k in range(4):
        small = jnp.where(lanes == SEND + k, sends[k], small)
    small = small.astype(jnp.float32).astype(jnp.bfloat16)
    for out, which in ((first, core), (second, 1 - core)):
        out[:INPUT, :] = weights[...]
        out[INPUT:SMALL, :] = feats[which]
        out[SMALL:, :] = small


def toward_inputs(table, even, odd, *outs):
    *toward, small = outs
    for slot, source in enumerate((even, odd)):
        for i, out in enumerate(toward):
            start = pl.multiple_of(INPUT + table[slot, SEND + 3 - i] * BLK, BLK)
            out[slot * BLK : (slot + 1) * BLK, :] = source[pl.ds(start, BLK), :]
    small[...] = even[SMALL:, :]


def mix_inputs(table, even, odd, h0, h1, h2, h3, mixed_even, mixed_odd, slots):
    for slot, (source, out) in enumerate(((even, mixed_even), (odd, mixed_odd))):
        slots[0] = source[INPUT : INPUT + BLK, :]
        slots[1] = source[INPUT + BLK : SMALL, :]
        for i, halo in zip(ORDER, (h0, h1, h2, h3)):
            slots[2 + i] = halo[slot * BLK : (slot + 1) * BLK, :]
        graph_product(table, slot, source, slots, out)


def input_gate(source, mixed, w_input, bias, cols):
    return (
        dot(source[INPUT:SMALL, :], w_input[0, :, cols])
        + dot(mixed[...], w_input[1, :, cols])
        + bias[:, cols]
    )


def first_step(table, source, mixed, w_input, bias, hidden, t0, t1, t2, t3):
    update = jax.nn.sigmoid(input_gate(source, mixed, w_input, bias, slice(0, HID)))
    candidate = jnp.tanh(input_gate(source, mixed, w_input, bias, slice(2 * HID, 3 * HID)))
    hidden[...] = ((1.0 - update) * candidate).astype(jnp.bfloat16)
    put_toward(table, 1, hidden, (t0, t1, t2, t3))


def early_gates(table, source, mixed, hidden, w_input, w_hidden, bias, gates):
    for column in range(3):
        cols = slice(column * HID, (column + 1) * HID)
        value = input_gate(source, mixed, w_input, bias, cols)
        if column < 2:
            value += dot(hidden[...], w_hidden[0, :, cols])
        gates[:, cols] = value


def reset_step(slot, table, hidden, h0, h1, h2, h3, source, gates, w_hidden, state, mixed, t0, t1, t2, t3, slots):
    fill(slots, hidden, (h0, h1, h2, h3))
    graph_product(table, slot, source, slots, mixed)
    reset = jax.nn.sigmoid(gates[:, HID : 2 * HID] + dot(mixed[...], w_hidden[1, :, HID:]))
    state[...] = (reset * hidden[...].astype(jnp.float32)).astype(jnp.bfloat16)
    put_toward(table, slot, state, (t0, t1, t2, t3))


def late_gates(table, gates, mixed, state, w_hidden, w_cand, update, partial):
    update[...] = jax.nn.sigmoid(gates[:, :HID] + dot(mixed[...], w_hidden[1, :, :HID]))
    partial[...] = gates[:, 2 * HID :] + dot(state[...], w_cand[0])


def new_hidden(slot, pair, last, table, hidden, state, h0, h1, h2, h3, source, update, partial, w_cand, kept_in, out, kept, *rest):
    *toward, slots, mixed = rest
    fill(slots, state, (h0, h1, h2, h3))
    graph_product(table, slot, source, slots, mixed)
    candidate = jnp.tanh(partial[...] + dot(mixed[...], w_cand[1]))
    gate = update[...]
    out[...] = (gate * hidden[...].astype(jnp.float32) + (1.0 - gate) * candidate).astype(jnp.bfloat16)
    if not last:
        put_toward(table, 1 + slot, out, toward)

    @pl.when(table[0, PAIR] == pair)
    def _():
        kept[...] = out[...]


def last_hidden(slot, pair, *refs):
    *inputs, kept, slots, mixed, out = refs
    new_hidden(slot, pair, True, *inputs, out, kept, slots, mixed)


def local(node_feats, adjacency, columns, send_list, w_input, w_hidden, w_cand, gate_bias):
    bf16, f32 = jnp.bfloat16, jnp.float32
    snap = lax.axis_index("tm")
    z, core = lax.axis_index("graph") % 8, snap % 2
    seq = z // 4
    bias = gate_bias[None, :]
    packed = pl.pallas_call(
        pack_inputs,
        out_shape=[jax.ShapeDtypeStruct((SMALL + 16, BLK), bf16)] * 2,
        in_specs=[SMEM] * 3 + [VMEM] * 2,
        out_specs=[VMEM] * 2,
        compiler_params=pltpu.CompilerParams(vmem_limit_bytes=12 << 20),
    )(columns.reshape(-1), send_list.reshape(-1), snap.reshape(1), adjacency.reshape(8 * BLK, BLK), node_feats[:, 0])
    got = [lax.ppermute(v, AXES, input_route(other)) for other, v in enumerate(packed)]
    even = jnp.where(seq == 0, got[0], got[1])
    odd = jnp.where(seq == 0, got[1], got[0])
    block = ((BLK, HID), bf16)
    full = ((ROWS, HID), bf16)
    wide = ((ROWS, HID), f32)
    slots = pltpu.VMEM((6, BLK, HID), bf16)

    def integers(*rows):
        return jnp.concatenate([r[:1] for r in rows], axis=0).astype(jnp.int32)

    def exchange(blocks, move=None):
        return [lax.ppermute(blocks[i], AXES, exchange_route(OFFSETS[i], move)) for i in ORDER]

    table = integers(even[SMALL:], odd[SMALL:])
    *toward, small = call(
        toward_inputs, table, (even, odd), [((2 * BLK, FEAT), bf16)] * 4 + [((16, 128), bf16)], 0
    )
    halos = exchange(toward)
    mixes = call(
        mix_inputs, table, (even, odd, *halos), [((ROWS, FEAT), bf16)] * 2, 2 * 2 * ROWS * 512 * FEAT,
        scratch=(pltpu.VMEM((6, BLK, FEAT), bf16),),
    )
    hidden, *toward = call(
        first_step, table, (even, mixes[0], w_input, bias), [full] + [block] * 4, 2 * ROWS * 256 * 1024
    )
    before = [(place(s, q, p), place(s, (q - 1) % 4, p)) for s, q, p in EVERY]
    small, hidden = lax.optimization_barrier((small, hidden))
    following = lax.ppermute(small, AXES, before)
    later_table = integers(even[SMALL:], odd[SMALL:], following)
    kept = [hidden, hidden]
    sources = (even, odd)
    for t in range(1, 8):
        slot, move = t % 2, {2: "swap", 4: "next", 6: "swap"}.get(t)
        if move:
            hidden = lax.ppermute(hidden, AXES, exchange_route(0, move))
        halos = exchange(toward, move)
        (gates,) = call(
            early_gates, table, (sources[slot], mixes[slot], hidden, w_input, w_hidden, bias), [((ROWS, 3 * HID), f32)],
            2 * ROWS * (256 * 1536 + 512 * 1024),
        )
        state, mixed_h, *toward = call(
            functools.partial(reset_step, slot), table, (hidden, *halos, sources[slot], gates, w_hidden),
            [full, full] + [block] * 4, 2 * ROWS * 512 * 1024, scratch=(slots,),
        )
        halos = exchange(toward)
        update, partial = call(
            late_gates, table, (gates, mixed_h, state, w_hidden, w_cand), [wide, wide], 2 * ROWS * 512 * 1024
        )
        operands = (hidden, state, *halos, sources[slot], update, partial, w_cand, kept[slot])
        held = pltpu.VMEM((ROWS, HID), bf16)
        if t == 7:
            (kept[slot],) = call(
                functools.partial(last_hidden, slot, t // 2), later_table, operands, [full], 2 * ROWS * 512 * 1024,
                scratch=(slots, held, held), aliases={11: 0},
            )
        else:
            hidden, kept[slot], *toward = call(
                functools.partial(new_hidden, slot, t // 2, False), later_table, operands,
                [full, full] + [block] * 4, 2 * ROWS * 512 * 1024, scratch=(slots, held), aliases={11: 1},
            )
    first = lax.ppermute(jnp.where(seq == 0, kept[0], kept[1]), AXES, output_route(0))
    second = lax.ppermute(jnp.where(seq == 0, kept[1], kept[0]), AXES, output_route(1))
    flip = core == 0
    return jnp.stack([jnp.where(flip, first, second), jnp.where(flip, second, first)])[:, None]


def solution(mesh):
    return jax.shard_map(
        local,
        mesh=mesh,
        in_specs=(
            P(None, "tm", "graph", None),
            P("tm", "graph", None, None, None),
            P("tm", "graph", None),
            P("tm", "graph", None),
            P(),
            P(),
            P(),
            P(),
        ),
        out_specs=P(None, "tm", "graph", None),
        check_vma=False,
    )
```
